768 devices in a mesh: energy: 24 (over x, z_lo, core), atom: 32 (over y, z_hi).
Axes of the slice: x: 4, y: 8, z: 12 (z_hi: 4, z_lo: 3; z = z_hi * 3 + z_lo), core: 2. Of those that a mesh axis runs over, the one named last changes fastest.
Arguments:
- green: float32 [2, 48, 64, 128, 128], P(None, 'energy', 'atom'), may hold values from -6 to 6
- coupling: float32 [64, 6, 128, 128], P('atom'), may hold values from -0.5 to 0.5
- phonon: float32 [64, 6, 4], P('atom'), may hold values from 0.2 to 2
- neighbours: int32 [64, 6], P('atom'), may hold values from 0 to 63, as said below
Outputs:
- self_energy: float32 [2, 48, 64, 128, 128], P(None, 'energy', 'atom')
- rates: float32 [64, 128], P('atom')
The draws below stay inside these ranges and needn't reach their ends.
Inputs may be any that keep to these rules, and one draw needn't show every extreme that they name: `neighbours`: each entry lies within 2 of its row's index and within 0 to 63; offsets +2 and -2 both occur.
All inputs are finite; a program needn't handle non-finite values.
Results may differ from the reference program's by a relative error of at most 0.000071.
Values sent between devices are 32-bit elements; how exact they have to be, the bound alone decides.
A program may use at most 32 MiB of HBM per device.

```python
import math
import jax
import jax.numpy as jnp
from jax import lax

ORB = 128
NBR = 6
NE = 48
NA = 64


def draw_neighbours(key, part):
    key_offsets, key_rows = jax.random.split(jax.random.fold_in(key, 17))
    offsets = jax.random.randint(key_offsets, (NA, NBR), -2, 3)
    picked = jax.random.randint(key_rows, (2,), 2, NA - 2)
    offsets = offsets.at[picked[0], 0].set(2)
    offsets = offsets.at[picked[1], 1].set(-2)
    base = jnp.arange(NA, dtype=jnp.int32)[:, None]
    return jnp.clip(base + offsets, 0, NA - 1).astype(jnp.int32)


def block_scale(key, dims, cuts, least, largest):
    def one(dim, shards_of):
        steps = jax.random.uniform(jax.random.fold_in(jax.random.fold_in(key, 6), dim), (shards_of,), jnp.float32, least / len(cuts), largest / len(cuts))
        return jnp.repeat(jnp.exp(steps), dims[dim] // shards_of).reshape((-1,) + (1,) * (len(dims) - dim - 1))

    level = one(*cuts[0])
    for cut in cuts[1:]:
        level = level * one(*cut)
    return level


def centred(rng, dims, scale, reach, pieces=(), kind=jnp.bfloat16):
    result = scale * jax.random.normal(rng, dims, jnp.float32)
    if pieces:
        result = result * block_scale(rng, dims, pieces, -0.22, 0.18)
    return jnp.clip(result, -reach, reach).astype(kind)


def setup_inputs(seed: int = 0) -> dict:
    arg_keys = jax.random.split(jax.random.key(seed), 5)
    green = centred(arg_keys[0], (2, NE, NA, ORB, ORB), 1.0, 6.0, ((1, 24), (2, 32)), jnp.float32)
    coupling = centred(arg_keys[1], (NA, NBR, ORB, ORB), ORB ** -0.5, 0.5, ((0, 32),), jnp.float32)
    phonon = jnp.clip(jnp.exp(math.log(2.0) - 2.3025851 * jax.random.uniform(arg_keys[2], (NA, NBR, 4), jnp.float32) ** block_scale(arg_keys[2], (NA, NBR, 4), ((0, 32),), -0.2, 0.2)), 0.2, 2.0)
    neighbours = draw_neighbours(jax.random.fold_in(arg_keys[4], 71), 0)
    return {"green": green, "coupling": coupling, "phonon": phonon, "neighbours": neighbours}


def reference(green, coupling, phonon, neighbours):
    highest = lax.Precision.HIGHEST
    shifts = (-2, -1, 1, 2)

    def one_block(index):
        rows = neighbours[index]
        near = jnp.take(green, rows, axis=2)
        padded = jnp.pad(near, ((0, 0), (2, 2), (0, 0), (0, 0), (0, 0)))
        mixed = jnp.zeros_like(near)
        for step in range(4):
            start = 2 + shifts[step]
            factor = phonon[index, :, step][None, None, :, None, None]
            mixed = mixed + factor * padded[:, start:start + NE]
        mats = coupling[index]
        inner = jnp.einsum('jik,cejkl->cejil', mats, mixed, precision=highest)
        sigma = jnp.einsum('cejil,jml->ceim', inner, mats, precision=highest)
        own = green[:, :, index]
        rate = jnp.einsum('eil,eli->i', sigma[0], own[0], precision=highest) - jnp.einsum('eil,eli->i', sigma[1], own[1], precision=highest)
        return sigma, rate / (4.0 * NE)

    sigmas, rates = lax.map(one_block, jnp.arange(NA, dtype=jnp.int32))
    self_energy = jnp.transpose(sigmas, (1, 2, 0, 3, 4))
    return self_energy, rates
```

```python
import functools

import jax
import jax.numpy as jnp
from jax import lax
from jax.experimental import pallas as pl
from jax.experimental.pallas import tpu as pltpu
from jax.sharding import PartitionSpec as P

MESH = pl.DeviceIdType.MESH
F32 = jnp.float32
BF16 = jnp.bfloat16


def split(x):
    high = x.astype(BF16)
    low = (x - high.astype(F32)).astype(BF16)
    return high, low


def kernel(
    n_energy,
    n_atom,
    nbr,
    orb,
    nbr_ref,
    ph_ref,
    green,
    coupling,
    sigma_out,
    rates_out,
    gbuf,
    cbuf,
    cleft,
    cright,
    gs,
    tbuf,
    own,
    send_next,
    send_prev,
    from_prev,
    from_next,
    gt,
    rsrc,
    rslots,
    local_sem,
    a_send,
    a_recv,
    u_send,
    u_recv,
    r_send,
    r_recv,
    o_sem,
):
    ei = lax.axis_index("energy")
    ai = lax.axis_index("atom")
    nxt_a, prv_a = lax.rem(ai + 1, n_atom), lax.rem(ai + n_atom - 1, n_atom)
    nxt_e, prv_e = lax.rem(ei + 1, n_energy), lax.rem(ei + n_energy - 1, n_energy)

    barrier = pltpu.get_barrier_semaphore()
    pl.semaphore_signal(barrier, inc=1, device_id={"atom": nxt_a}, device_id_type=MESH)
    pl.semaphore_signal(barrier, inc=1, device_id={"atom": prv_a}, device_id_type=MESH)

    def greet(p, carry):
        peer = lax.rem(ei + p, n_energy)
        pl.semaphore_signal(barrier, inc=1, device_id={"energy": peer}, device_id_type=MESH)
        return carry

    lax.fori_loop(1, n_energy, greet, 0)

    load_c = pltpu.make_async_copy(coupling, cbuf, local_sem.at[0])
    load_g = pltpu.make_async_copy(green, gbuf.at[:, :, pl.ds(2, 2)], local_sem.at[1])
    load_c.start()
    load_g.start()

    pl.semaphore_wait(barrier, n_energy + 1)

    def atom_copy(c, e, up):
        return pltpu.make_async_remote_copy(
            src_ref=green.at[c, e],
            dst_ref=gbuf.at[c, e, pl.ds(0 if up else 4, 2)],
            send_sem=a_send.at[int(up), c * 2 + e],
            recv_sem=a_recv.at[int(up), c * 2 + e],
            device_id={"atom": nxt_a if up else prv_a},
            device_id_type=MESH,
        )

    for c in range(2):
        for e in range(2):
            atom_copy(c, e, True).start()
            atom_copy(c, e, False).start()

    def energy_copy(c, e, a, up):
        index = (c * 2 + e) * 2 + a
        return pltpu.make_async_remote_copy(
            src_ref=(send_next if up else send_prev).at[c, e, a],
            dst_ref=(from_prev if up else from_next).at[c, e, a],
            send_sem=u_send.at[int(up), index],
            recv_sem=u_recv.at[int(up), index],
            device_id={"energy": nxt_e if up else prv_e},
            device_id_type=MESH,
        )

    load_c.wait()

    def prepare(i, carry):
        mat = cbuf[i]
        high, low = split(mat)
        cleft[i, :, :orb] = high
        cleft[i, :, orb:] = low
        high, low = split(mat.T)
        for row in range(2):
            cright[i, row * orb : (row + 1) * orb, :orb] = high
            cright[i, row * orb : (row + 1) * orb, orb:] = low
        return carry

    lax.fori_loop(0, 2 * nbr, prepare, 0)
    load_g.wait()

    def turn(i, carry):
        c, e, a = i // 4, (i // 2) % 2, i % 2
        gt[c, e, a] = gbuf[c, e, 2 + a].T
        return carry

    lax.fori_loop(0, 8, turn, 0)

    first = ai * 2

    def fill(c, e):
        def body(b, carry):
            high, low = split(gbuf[c, e, b])
            for row in range(2):
                gs[b, row * orb : (row + 1) * orb, :orb] = high
                gs[b, row * orb : (row + 1) * orb, orb:] = low
            return carry

        lax.fori_loop(0, 6, body, 0)

    def products(a):
        for j in range(nbr):
            i = a * nbr + j
            near = jnp.clip(nbr_ref[i] - first + 2, 0, 5)
            both = jnp.dot(cleft[i], gs[near], preferred_element_type=F32)
            high, low = split(both[:, :orb] + both[:, orb:])
            inner = jnp.concatenate([high, low], axis=1)
            both = jnp.dot(inner, cright[i], preferred_element_type=F32)
            tbuf[j] = both[:, :orb] + both[:, orb:]

    def mix(a, targets):
        weights = [[ph_ref[(a * nbr + j) * 4 + k] for k in range(4)] for j in range(nbr)]
        rows = 32

        def body(r, carry):
            at = pl.ds(pl.multiple_of(r * rows, rows), rows)
            terms = [tbuf[j, at, :] for j in range(nbr)]
            for k in range(4):
                ref, add = targets[k]
                total = weights[0][k] * terms[0]
                for j in range(1, nbr):
                    total = total + weights[j][k] * terms[j]
                if add:
                    total = total + ref[at, :]
                ref[at, :] = total
            return carry

        lax.fori_loop(0, orb // rows, body, 0)

    def one_c(c, carry):
        for e in range(2):
            atom_copy(c, e, True).wait_recv()
            atom_copy(c, e, False).wait_recv()
            fill(c, e)

            def one_a(a, inner_carry):
                products(a)
                if e == 0:
                    mix(
                        a,
                        (
                            (send_next.at[c, 0, a], False),
                            (own.at[c, 1, a], False),
                            (send_prev.at[c, 1, a], False),
                            (send_prev.at[c, 0, a], False),
                        ),
                    )
                    energy_copy(c, 0, a, False).start()
                else:
                    mix(
                        a,
                        (
                            (send_next.at[c, 1, a], False),
                            (send_next.at[c, 0, a], True),
                            (own.at[c, 0, a], False),
                            (send_prev.at[c, 1, a], True),
                        ),
                    )
                    energy_copy(c, 0, a, True).start()
                    energy_copy(c, 1, a, True).start()
                    energy_copy(c, 1, a, False).start()
                return inner_carry

            lax.fori_loop(0, 2, one_a, 0)
        return carry

    lax.fori_loop(0, 2, one_c, 0)

    has_prev, has_next = ei > 0, ei < n_energy - 1
    rsrc[...] = jnp.zeros_like(rsrc)

    def out_copy(c, e, a):
        return pltpu.make_async_copy(
            own.at[c, e, a], sigma_out.at[c, e, a], o_sem.at[(c * 2 + e) * 2 + a]
        )

    for a in range(2):
        total = jnp.zeros((orb, orb), F32)
        for c in range(2):
            for e in range(2):
                energy_copy(c, e, a, True).wait_recv()
                energy_copy(c, e, a, False).wait_recv()
                block = own[c, e, a]
                block = block + jnp.where(has_prev, from_prev[c, e, a], 0.0)
                block = block + jnp.where(has_next, from_next[c, e, a], 0.0)
                own[c, e, a] = block
                term = block * gt[c, e, a]
                total = total + term if c == 0 else total - term
                out_copy(c, e, a).start()
        rsrc[a : a + 1, :] = jnp.sum(total.T, axis=0, keepdims=True)

    def rate_copy(sender, target):
        return pltpu.make_async_remote_copy(
            src_ref=rsrc,
            dst_ref=rslots.at[sender],
            send_sem=r_send.at[target],
            recv_sem=r_recv.at[sender],
            device_id={"energy": target},
            device_id_type=MESH,
        )

    def send_rate(p, carry):
        rate_copy(ei, lax.rem(ei + p, n_energy)).start()
        return carry

    lax.fori_loop(1, n_energy, send_rate, 0)
    rslots[ei] = rsrc[...]

    def wait_rate(p, carry):
        peer = lax.rem(ei + p, n_energy)
        rate_copy(peer, peer).wait_recv()
        return carry

    lax.fori_loop(1, n_energy, wait_rate, 0)
    total = rslots[0]
    for s in range(1, n_energy):
        total = total + rslots[s]
    rates_out[...] = total[:2] * (1.0 / (4.0 * 2 * n_energy))

    for c in range(2):
        for e in range(2):
            atom_copy(c, e, True).wait_send()
            atom_copy(c, e, False).wait_send()
            for a in range(2):
                energy_copy(c, e, a, True).wait_send()
                energy_copy(c, e, a, False).wait_send()
                out_copy(c, e, a).wait()

    def wait_rate_send(p, carry):
        rate_copy(ei, lax.rem(ei + p, n_energy)).wait_send()
        return carry

    lax.fori_loop(1, n_energy, wait_rate_send, 0)


def solution(mesh):
    n_energy, n_atom = mesh.shape["energy"], mesh.shape["atom"]

    def per_device(green, coupling, phonon, neighbours):
        orb, nbr = green.shape[-1], coupling.shape[1]
        rows = 2 * nbr
        whole = (2, 2, 2, orb, orb)
        any_space = pl.BlockSpec(memory_space=pl.ANY)
        smem = pl.BlockSpec(memory_space=pltpu.SMEM)
        sigma, rates = pl.pallas_call(
            functools.partial(kernel, n_energy, n_atom, nbr, orb),
            out_shape=(
                jax.ShapeDtypeStruct(whole, F32),
                jax.ShapeDtypeStruct((2, orb), F32),
            ),
            in_specs=[smem, smem, any_space, any_space],
            out_specs=(any_space, pl.BlockSpec(memory_space=pltpu.VMEM)),
            scratch_shapes=[
                pltpu.VMEM((2, 2, 6, orb, orb), F32),
                pltpu.VMEM((rows, orb, orb), F32),
                pltpu.VMEM((rows, orb, 2 * orb), BF16),
                pltpu.VMEM((rows, 2 * orb, 2 * orb), BF16),
                pltpu.VMEM((6, 2 * orb, 2 * orb), BF16),
                pltpu.VMEM((nbr, orb, orb), F32),
                pltpu.VMEM(whole, F32),
                pltpu.VMEM(whole, F32),
                pltpu.VMEM(whole, F32),
                pltpu.VMEM(whole, F32),
                pltpu.VMEM(whole, F32),
                pltpu.VMEM(whole, F32),
                pltpu.VMEM((8, orb), F32),
                pltpu.VMEM((n_energy, 8, orb), F32),
                pltpu.SemaphoreType.DMA((2,)),
                pltpu.SemaphoreType.DMA((2, 4)),
                pltpu.SemaphoreType.DMA((2, 4)),
                pltpu.SemaphoreType.DMA((2, 8)),
                pltpu.SemaphoreType.DMA((2, 8)),
                pltpu.SemaphoreType.DMA((n_energy,)),
                pltpu.SemaphoreType.DMA((n_energy,)),
                pltpu.SemaphoreType.DMA((8,)),
            ],
            compiler_params=pltpu.CompilerParams(collective_id=0, has_side_effects=True),
            name="self_energy",
        )(
            neighbours.reshape(rows),
            phonon.reshape(rows * 4),
            green,
            coupling.reshape(rows, orb, orb),
        )
        return sigma, rates

    return jax.shard_map(
        per_device,
        mesh=mesh,
        in_specs=(
            P(None, "energy", "atom", None, None),
            P("atom", None, None, None),
            P("atom", None, None),
            P("atom", None),
        ),
        out_specs=(P(None, "energy", "atom", None, None), P("atom", None)),
        check_vma=False,
    )
```

```python
import functools

import jax
import jax.numpy as jnp
from jax import lax
from jax.experimental import pallas as pl
from jax.experimental.pallas import tpu as pltpu
from jax.sharding import PartitionSpec as P

MESH = pl.DeviceIdType.MESH
F32 = jnp.float32
BF16 = jnp.bfloat16


def split(x):
    high = x.astype(BF16)
    low = (x - high.astype(F32)).astype(BF16)
    return high, low


def kernel(
    n_energy,
    n_atom,
    nbr,
    orb,
    nbr_hbm,
    ph_hbm,
    green,
    coupling,
    sigma_out,
    rates_out,
    nbr_ref,
    ph_ref,
    gbuf,
    cbuf,
    cleft,
    cright,
    gs,
    tbuf,
    own,
    send_next,
    send_prev,
    from_prev,
    from_next,
    gt,
    rsrc,
    rslots,
    local_sem,
    ready,
    known,
    a_send,
    a_recv,
    u_send,
    u_recv,
    r_send,
    r_recv,
    o_sem,
):
    ei = lax.axis_index("energy")
    ai = lax.axis_index("atom")
    nxt_a, prv_a = lax.rem(ai + 1, n_atom), lax.rem(ai + n_atom - 1, n_atom)
    nxt_e, prv_e = lax.rem(ei + 1, n_energy), lax.rem(ei + n_energy - 1, n_energy)

    barrier = pltpu.get_barrier_semaphore()
    pl.semaphore_signal(barrier, inc=1, device_id={"atom": prv_a}, device_id_type=MESH)
    pl.semaphore_signal(barrier, inc=1, device_id={"energy": prv_e}, device_id_type=MESH)

    load_n = pltpu.make_async_copy(nbr_hbm, nbr_ref, local_sem.at[2])
    load_p = pltpu.make_async_copy(ph_hbm, ph_ref, local_sem.at[3])
    load_c = pltpu.make_async_copy(coupling, cbuf, local_sem.at[0])
    load_g = pltpu.make_async_copy(green, gbuf.at[:, :, pl.ds(2, 2)], local_sem.at[1])
    load_n.start()
    load_p.start()
    load_c.start()
    load_g.start()

    not_last, not_first = ai < n_atom - 1, ai > 0

    def atom_copy(c, e, up):
        return pltpu.make_async_remote_copy(
            src_ref=green.at[c, e],
            dst_ref=gbuf.at[c, e, pl.ds(0 if up else 4, 2)],
            send_sem=a_send.at[int(up), c * 2 + e],
            recv_sem=a_recv.at[int(up), c * 2 + e],
            device_id={"atom": nxt_a if up else prv_a},
            device_id_type=MESH,
        )

    pl.semaphore_wait(barrier, 2)
    pl.semaphore_signal(ready.at[0], inc=1, device_id={"atom": nxt_a}, device_id_type=MESH)
    pl.semaphore_signal(ready.at[1], inc=1, device_id={"energy": nxt_e}, device_id_type=MESH)

    @pl.when(not_last)
    def _():
        for c in range(2):
            for e in range(2):
                atom_copy(c, e, True).start()

    load_c.wait()

    def prepare(i, carry):
        mat = cbuf[i]
        high, low = split(mat)
        cleft[i, :, :orb] = high
        cleft[i, :, orb:] = low
        high, low = split(mat.T)
        for row in range(2):
            cright[i, row * orb : (row + 1) * orb, :orb] = high
            cright[i, row * orb : (row + 1) * orb, orb:] = low
        return carry

    lax.fori_loop(0, 2 * nbr, prepare, 0)

    pl.semaphore_wait(ready.at[0], 1)

    @pl.when(not_first)
    def _():
        for c in range(2):
            for e in range(2):
                atom_copy(c, e, False).start()

    pl.semaphore_wait(ready.at[1], 1)

    def tell(r):
        reach = 2**r
        for side, peer in enumerate((ei + reach, ei + n_energy - reach)):
            pl.semaphore_signal(
                known.at[side, r],
                inc=1,
                device_id={"energy": lax.rem(peer, n_energy)},
                device_id_type=MESH,
            )

    def hear(r):
        pl.semaphore_wait(known.at[0, r], 1)
        pl.semaphore_wait(known.at[1, r], 1)

    rounds = (n_energy // 2 - 1).bit_length()
    tell(0)
    load_g.wait()

    def turn(i, carry):
        c, e, a = i // 4, (i // 2) % 2, i % 2
        gt[c, e, a] = gbuf[c, e, 2 + a].T
        return carry

    lax.fori_loop(0, 8, turn, 0)
    load_n.wait()
    load_p.wait()
    for r in range(1, rounds):
        hear(r - 1)
        tell(r)
    hear(rounds - 1)

    def energy_copy(c, e, a, up):
        index = (c * 2 + e) * 2 + a
        return pltpu.make_async_remote_copy(
            src_ref=(send_next if up else send_prev).at[c, e, a],
            dst_ref=(from_prev if up else from_next).at[c, e, a],
            send_sem=u_send.at[int(up), index],
            recv_sem=u_recv.at[int(up), index],
            device_id={"energy": nxt_e if up else prv_e},
            device_id_type=MESH,
        )

    first = ai * 2

    def fill(c, e):
        def body(b, carry):
            high, low = split(gbuf[c, e, b])
            for row in range(2):
                gs[b, row * orb : (row + 1) * orb, :orb] = high
                gs[b, row * orb : (row + 1) * orb, orb:] = low
            return carry

        lax.fori_loop(0, 6, body, 0)

    def products(a):
        for j in range(nbr):
            i = a * nbr + j
            near = jnp.clip(nbr_ref[a, j] - first + 2, 0, 5)
            both = jnp.dot(cleft[i], gs[near], preferred_element_type=F32)
            high, low = split(both[:, :orb] + both[:, orb:])
            inner = jnp.concatenate([high, low], axis=1)
            both = jnp.dot(inner, cright[i], preferred_element_type=F32)
            tbuf[j] = both[:, :orb] + both[:, orb:]

    def mix(a, targets):
        weights = [[ph_ref[a, k, j] for k in range(4)] for j in range(nbr)]
        rows = 32

        def body(r, carry):
            at = pl.ds(pl.multiple_of(r * rows, rows), rows)
            terms = [tbuf[j, at, :] for j in range(nbr)]
            for k in range(4):
                ref, add = targets[k]
                total = weights[0][k] * terms[0]
                for j in range(1, nbr):
                    total = total + weights[j][k] * terms[j]
                if add:
                    total = total + ref[at, :]
                ref[at, :] = total
            return carry

        lax.fori_loop(0, orb // rows, body, 0)

    def one_c(c, carry):
        for e in range(2):
            @pl.when(not_first)
            def _():
                atom_copy(c, e, True).wait_recv()

            @pl.when(not_last)
            def _():
                atom_copy(c, e, False).wait_recv()

            fill(c, e)

            def one_a(a, inner_carry):
                products(a)
                if e == 0:
                    mix(
                        a,
                        (
                            (send_next.at[c, 0, a], False),
                            (own.at[c, 1, a], False),
                            (send_prev.at[c, 1, a], False),
                            (send_prev.at[c, 0, a], False),
                        ),
                    )
                    energy_copy(c, 0, a, False).start()
                else:
                    mix(
                        a,
                        (
                            (send_next.at[c, 1, a], False),
                            (send_next.at[c, 0, a], True),
                            (own.at[c, 0, a], False),
                            (send_prev.at[c, 1, a], True),
                        ),
                    )
                    energy_copy(c, 0, a, True).start()
                    energy_copy(c, 1, a, True).start()
                    energy_copy(c, 1, a, False).start()
                return inner_carry

            lax.fori_loop(0, 2, one_a, 0)
        return carry

    lax.fori_loop(0, 2, one_c, 0)

    has_prev, has_next = ei > 0, ei < n_energy - 1
    rsrc[...] = jnp.zeros_like(rsrc)

    def out_copy(c, e, a):
        return pltpu.make_async_copy(
            own.at[c, e, a], sigma_out.at[c, e, a], o_sem.at[(c * 2 + e) * 2 + a]
        )

    for a in range(2):
        total = jnp.zeros((orb, orb), F32)
        for c in range(2):
            for e in range(2):
                energy_copy(c, e, a, True).wait_recv()
                energy_copy(c, e, a, False).wait_recv()
                block = own[c, e, a]
                block = block + jnp.where(has_prev, from_prev[c, e, a], 0.0)
                block = block + jnp.where(has_next, from_next[c, e, a], 0.0)
                own[c, e, a] = block
                term = block * gt[c, e, a]
                total = total + term if c == 0 else total - term
                out_copy(c, e, a).start()
        rsrc[a : a + 1, :] = jnp.sum(total.T, axis=0, keepdims=True)

    def rate_copy(sender, target):
        return pltpu.make_async_remote_copy(
            src_ref=rsrc,
            dst_ref=rslots.at[sender],
            send_sem=r_send.at[target],
            recv_sem=r_recv.at[sender],
            device_id={"energy": target},
            device_id_type=MESH,
        )

    def send_rate(p, carry):
        rate_copy(ei, lax.rem(ei + p, n_energy)).start()
        return carry

    lax.fori_loop(1, n_energy, send_rate, 0)
    rslots[ei] = rsrc[...]

    def wait_rate(p, carry):
        peer = lax.rem(ei + p, n_energy)
        rate_copy(peer, peer).wait_recv()
        return carry

    lax.fori_loop(1, n_energy, wait_rate, 0)
    total = rslots[0]
    for s in range(1, n_energy):
        total = total + rslots[s]
    rates_out[...] = total[:2] * (1.0 / (4.0 * 2 * n_energy))

    for c in range(2):
        for e in range(2):
            @pl.when(not_last)
            def _():
                atom_copy(c, e, True).wait_send()

            @pl.when(not_first)
            def _():
                atom_copy(c, e, False).wait_send()

            for a in range(2):
                energy_copy(c, e, a, True).wait_send()
                energy_copy(c, e, a, False).wait_send()
                out_copy(c, e, a).wait()

    def wait_rate_send(p, carry):
        rate_copy(ei, lax.rem(ei + p, n_energy)).wait_send()
        return carry

    lax.fori_loop(1, n_energy, wait_rate_send, 0)


def solution(mesh):
    n_energy, n_atom = mesh.shape["energy"], mesh.shape["atom"]

    def per_device(green, coupling, phonon, neighbours):
        orb, nbr = green.shape[-1], coupling.shape[1]
        rows = 2 * nbr
        whole = (2, 2, 2, orb, orb)
        any_space = pl.BlockSpec(memory_space=pl.ANY)
        sigma, rates = pl.pallas_call(
            functools.partial(kernel, n_energy, n_atom, nbr, orb),
            out_shape=(
                jax.ShapeDtypeStruct(whole, F32),
                jax.ShapeDtypeStruct((2, orb), F32),
            ),
            in_specs=[any_space] * 4,
            out_specs=(any_space, pl.BlockSpec(memory_space=pltpu.VMEM)),
            scratch_shapes=[
                pltpu.SMEM((2, nbr), jnp.int32),
                pltpu.SMEM((2, 4, nbr), F32),
                pltpu.VMEM((2, 2, 6, orb, orb), F32),
                pltpu.VMEM((rows, orb, orb), F32),
                pltpu.VMEM((rows, orb, 2 * orb), BF16),
                pltpu.VMEM((rows, 2 * orb, 2 * orb), BF16),
                pltpu.VMEM((6, 2 * orb, 2 * orb), BF16),
                pltpu.VMEM((nbr, orb, orb), F32),
                pltpu.VMEM(whole, F32),
                pltpu.VMEM(whole, F32),
                pltpu.VMEM(whole, F32),
                pltpu.VMEM(whole, F32),
                pltpu.VMEM(whole, F32),
                pltpu.VMEM(whole, F32),
                pltpu.VMEM((8, orb), F32),
                pltpu.VMEM((n_energy, 8, orb), F32),
                pltpu.SemaphoreType.DMA((4,)),
                pltpu.SemaphoreType.REGULAR((2,)),
                pltpu.SemaphoreType.REGULAR((2, 8)),
                pltpu.SemaphoreType.DMA((2, 4)),
                pltpu.SemaphoreType.DMA((2, 4)),
                pltpu.SemaphoreType.DMA((2, 8)),
                pltpu.SemaphoreType.DMA((2, 8)),
                pltpu.SemaphoreType.DMA((n_energy,)),
                pltpu.SemaphoreType.DMA((n_energy,)),
                pltpu.SemaphoreType.DMA((8,)),
            ],
            compiler_params=pltpu.CompilerParams(collective_id=0, has_side_effects=True),
            name="self_energy",
        )(
            neighbours,
            jnp.transpose(phonon, (0, 2, 1)),
            green,
            coupling.reshape(rows, orb, orb),
        )
        return sigma, rates

    return jax.shard_map(
        per_device,
        mesh=mesh,
        in_specs=(
            P(None, "energy", "atom", None, None),
            P("atom", None, None, None),
            P("atom", None, None),
            P("atom", None),
        ),
        out_specs=(P(None, "energy", "atom", None, None), P("atom", None)),
        check_vma=False,
    )
```

```python
import functools

import jax
import jax.numpy as jnp
from jax import lax
from jax.experimental import pallas as pl
from jax.experimental.pallas import tpu as pltpu
from jax.sharding import PartitionSpec as P

MESH = pl.DeviceIdType.MESH
F32 = jnp.float32
BF16 = jnp.bfloat16
Z_GROUPS = 4


def split(x):
    high = x.astype(BF16)
    low = (x - high.astype(F32)).astype(BF16)
    return high, low


def kernel(
    n_energy,
    n_atom,
    nbr,
    orb,
    nbr_hbm,
    ph_hbm,
    green,
    coupling,
    sigma_out,
    rates_out,
    nbr_ref,
    ph_ref,
    gbuf,
    cbuf,
    cleft,
    cright,
    gs,
    tbuf,
    own,
    send_next,
    send_prev,
    from_prev,
    from_next,
    gt,
    rsrc,
    rslots,
    local_sem,
    ready,
    known,
    a_send,
    a_recv,
    u_send,
    u_recv,
    r_send,
    r_recv,
    o_sem,
):
    ei = lax.axis_index("energy")
    ai = lax.axis_index("atom")
    nxt_a, prv_a = lax.rem(ai + 1, n_atom), lax.rem(ai + n_atom - 1, n_atom)
    nxt_e, prv_e = lax.rem(ei + 1, n_energy), lax.rem(ei + n_energy - 1, n_energy)

    group = lax.rem(ai, Z_GROUPS)
    first_group, last_group = group == 0, group == Z_GROUPS - 1
    barrier = pltpu.get_barrier_semaphore()

    def greet(sem, axis, peer):
        pl.semaphore_signal(sem, inc=1, device_id={axis: peer}, device_id_type=MESH)

    greet(barrier, "energy", prv_e)

    @pl.when(jnp.logical_not(last_group))
    def _():
        greet(barrier, "atom", nxt_a)

    @pl.when(first_group)
    def _():
        greet(barrier, "atom", prv_a)

    load_n = pltpu.make_async_copy(nbr_hbm, nbr_ref, local_sem.at[2])
    load_p = pltpu.make_async_copy(ph_hbm, ph_ref, local_sem.at[3])
    load_c = pltpu.make_async_copy(coupling, cbuf, local_sem.at[0])
    load_g = pltpu.make_async_copy(green, gbuf.at[:, :, pl.ds(2, 2)], local_sem.at[1])
    load_n.start()
    load_p.start()
    load_c.start()
    load_g.start()

    not_last, not_first = ai < n_atom - 1, ai > 0

    def atom_copy(c, e, up):
        return pltpu.make_async_remote_copy(
            src_ref=green.at[c, e],
            dst_ref=gbuf.at[c, e, pl.ds(0 if up else 4, 2)],
            send_sem=a_send.at[int(up), c * 2 + e],
            recv_sem=a_recv.at[int(up), c * 2 + e],
            device_id={"atom": nxt_a if up else prv_a},
            device_id_type=MESH,
        )

    def send_up():
        @pl.when(not_last)
        def _():
            for c in range(2):
                for e in range(2):
                    atom_copy(c, e, True).start()

    def send_down(c, e):
        @pl.when(not_first)
        def _():
            atom_copy(c, e, False).start()

    @pl.when(first_group)
    def _():
        pl.semaphore_wait(barrier, 1)

    @pl.when(jnp.logical_and(jnp.logical_not(first_group), jnp.logical_not(last_group)))
    def _():
        pl.semaphore_wait(barrier, 2)

    @pl.when(last_group)
    def _():
        pl.semaphore_wait(barrier, 3)
        greet(ready.at[0], "atom", nxt_a)
        send_up()

    greet(ready.at[2], "energy", nxt_e)

    @pl.when(jnp.logical_not(first_group))
    def _():
        greet(ready.at[1], "atom", prv_a)
        for c in range(2):
            for e in range(2):
                send_down(c, e)

    @pl.when(first_group)
    def _():
        pl.semaphore_wait(ready.at[1], 1)
        send_up()

    load_c.wait()

    def prepare(i, carry):
        mat = cbuf[i]
        high, low = split(mat)
        cleft[i, :, :orb] = high
        cleft[i, :, orb:] = low
        high, low = split(mat.T)
        for row in range(2):
            cright[i, row * orb : (row + 1) * orb, :orb] = high
            cright[i, row * orb : (row + 1) * orb, orb:] = low
        return carry

    lax.fori_loop(0, 2 * nbr, prepare, 0)

    @pl.when(jnp.logical_and(jnp.logical_not(first_group), jnp.logical_not(last_group)))
    def _():
        pl.semaphore_wait(ready.at[1], 1)
        send_up()

    @pl.when(first_group)
    def _():
        pl.semaphore_wait(ready.at[0], 1)
        for c in range(2):
            for e in range(2):
                send_down(c, e)

    pl.semaphore_wait(ready.at[2], 1)

    def tell(r):
        reach = 2**r
        for side, peer in enumerate((ei + reach, ei + n_energy - reach)):
            pl.semaphore_signal(
                known.at[side, r],
                inc=1,
                device_id={"energy": lax.rem(peer, n_energy)},
                device_id_type=MESH,
            )

    def hear(r):
        pl.semaphore_wait(known.at[0, r], 1)
        pl.semaphore_wait(known.at[1, r], 1)

    rounds = (n_energy // 2 - 1).bit_length()
    tell(0)
    load_g.wait()

    def turn(i, carry):
        c, e, a = i // 4, (i // 2) % 2, i % 2
        gt[c, e, a] = gbuf[c, e, 2 + a].T
        return carry

    lax.fori_loop(0, 8, turn, 0)
    load_n.wait()
    load_p.wait()
    for r in range(1, rounds):
        hear(r - 1)
        tell(r)
    hear(rounds - 1)

    def energy_copy(c, e, a, up):
        index = (c * 2 + e) * 2 + a
        return pltpu.make_async_remote_copy(
            src_ref=(send_next if up else send_prev).at[c, e, a],
            dst_ref=(from_prev if up else from_next).at[c, e, a],
            send_sem=u_send.at[int(up), index],
            recv_sem=u_recv.at[int(up), index],
            device_id={"energy": nxt_e if up else prv_e},
            device_id_type=MESH,
        )

    first = ai * 2

    def fill(c, e):
        def body(b, carry):
            high, low = split(gbuf[c, e, b])
            for row in range(2):
                gs[b, row * orb : (row + 1) * orb, :orb] = high
                gs[b, row * orb : (row + 1) * orb, orb:] = low
            return carry

        lax.fori_loop(0, 6, body, 0)

    def products(a):
        for j in range(nbr):
            i = a * nbr + j
            near = jnp.clip(nbr_ref[a, j] - first + 2, 0, 5)
            both = jnp.dot(cleft[i], gs[near], preferred_element_type=F32)
            high, low = split(both[:, :orb] + both[:, orb:])
            inner = jnp.concatenate([high, low], axis=1)
            both = jnp.dot(inner, cright[i], preferred_element_type=F32)
            tbuf[j] = both[:, :orb] + both[:, orb:]

    def mix(a, targets):
        weights = [[ph_ref[a, k, j] for k in range(4)] for j in range(nbr)]
        rows = 32

        def body(r, carry):
            at = pl.ds(pl.multiple_of(r * rows, rows), rows)
            terms = [tbuf[j, at, :] for j in range(nbr)]
            for k in range(4):
                ref, add = targets[k]
                total = weights[0][k] * terms[0]
                for j in range(1, nbr):
                    total = total + weights[j][k] * terms[j]
                if add:
                    total = total + ref[at, :]
                ref[at, :] = total
            return carry

        lax.fori_loop(0, orb // rows, body, 0)

    def one_c(c, carry):
        for e in range(2):
            @pl.when(not_first)
            def _():
                atom_copy(c, e, True).wait_recv()

            @pl.when(not_last)
            def _():
                atom_copy(c, e, False).wait_recv()

            fill(c, e)

            def one_a(a, inner_carry):
                products(a)
                if e == 0:
                    mix(
                        a,
                        (
                            (send_next.at[c, 0, a], False),
                            (own.at[c, 1, a], False),
                            (send_prev.at[c, 1, a], False),
                            (send_prev.at[c, 0, a], False),
                        ),
                    )
                    energy_copy(c, 0, a, False).start()
                else:
                    mix(
                        a,
                        (
                            (send_next.at[c, 1, a], False),
                            (send_next.at[c, 0, a], True),
                            (own.at[c, 0, a], False),
                            (send_prev.at[c, 1, a], True),
                        ),
                    )
                    energy_copy(c, 0, a, True).start()
                    energy_copy(c, 1, a, True).start()
                    energy_copy(c, 1, a, False).start()
                return inner_carry

            lax.fori_loop(0, 2, one_a, 0)

        return carry

    lax.fori_loop(0, 2, one_c, 0)

    has_prev, has_next = ei > 0, ei < n_energy - 1
    rsrc[...] = jnp.zeros_like(rsrc)

    def out_copy(c, e, a):
        return pltpu.make_async_copy(
            own.at[c, e, a], sigma_out.at[c, e, a], o_sem.at[(c * 2 + e) * 2 + a]
        )

    for a in range(2):
        total = jnp.zeros((orb, orb), F32)
        for c in range(2):
            for e in range(2):
                energy_copy(c, e, a, True).wait_recv()
                energy_copy(c, e, a, False).wait_recv()
                block = own[c, e, a]
                block = block + jnp.where(has_prev, from_prev[c, e, a], 0.0)
                block = block + jnp.where(has_next, from_next[c, e, a], 0.0)
                own[c, e, a] = block
                term = block * gt[c, e, a]
                total = total + term if c == 0 else total - term
                out_copy(c, e, a).start()
        rsrc[a : a + 1, :] = jnp.sum(total.T, axis=0, keepdims=True)

    def rate_copy(sender, target):
        return pltpu.make_async_remote_copy(
            src_ref=rsrc,
            dst_ref=rslots.at[sender],
            send_sem=r_send.at[target],
            recv_sem=r_recv.at[sender],
            device_id={"energy": target},
            device_id_type=MESH,
        )

    def send_rate(p, carry):
        rate_copy(ei, lax.rem(ei + p, n_energy)).start()
        return carry

    lax.fori_loop(1, n_energy, send_rate, 0)
    rslots[ei] = rsrc[...]

    def wait_rate(p, carry):
        peer = lax.rem(ei + p, n_energy)
        rate_copy(peer, peer).wait_recv()
        return carry

    lax.fori_loop(1, n_energy, wait_rate, 0)
    total = rslots[0]
    for s in range(1, n_energy):
        total = total + rslots[s]
    rates_out[...] = total[:2] * (1.0 / (4.0 * 2 * n_energy))

    for c in range(2):
        for e in range(2):
            @pl.when(not_last)
            def _():
                atom_copy(c, e, True).wait_send()

            @pl.when(not_first)
            def _():
                atom_copy(c, e, False).wait_send()

            for a in range(2):
                energy_copy(c, e, a, True).wait_send()
                energy_copy(c, e, a, False).wait_send()
                out_copy(c, e, a).wait()

    def wait_rate_send(p, carry):
        rate_copy(ei, lax.rem(ei + p, n_energy)).wait_send()
        return carry

    lax.fori_loop(1, n_energy, wait_rate_send, 0)


def solution(mesh):
    n_energy, n_atom = mesh.shape["energy"], mesh.shape["atom"]

    def per_device(green, coupling, phonon, neighbours):
        orb, nbr = green.shape[-1], coupling.shape[1]
        rows = 2 * nbr
        whole = (2, 2, 2, orb, orb)
        any_space = pl.BlockSpec(memory_space=pl.ANY)
        sigma, rates = pl.pallas_call(
            functools.partial(kernel, n_energy, n_atom, nbr, orb),
            out_shape=(
                jax.ShapeDtypeStruct(whole, F32),
                jax.ShapeDtypeStruct((2, orb), F32),
            ),
            in_specs=[any_space] * 4,
            out_specs=(any_space, pl.BlockSpec(memory_space=pltpu.VMEM)),
            scratch_shapes=[
                pltpu.SMEM((2, nbr), jnp.int32),
                pltpu.SMEM((2, 4, nbr), F32),
                pltpu.VMEM((2, 2, 6, orb, orb), F32),
                pltpu.VMEM((rows, orb, orb), F32),
                pltpu.VMEM((rows, orb, 2 * orb), BF16),
                pltpu.VMEM((rows, 2 * orb, 2 * orb), BF16),
                pltpu.VMEM((6, 2 * orb, 2 * orb), BF16),
                pltpu.VMEM((nbr, orb, orb), F32),
                pltpu.VMEM(whole, F32),
                pltpu.VMEM(whole, F32),
                pltpu.VMEM(whole, F32),
                pltpu.VMEM(whole, F32),
                pltpu.VMEM(whole, F32),
                pltpu.VMEM(whole, F32),
                pltpu.VMEM((8, orb), F32),
                pltpu.VMEM((n_energy, 8, orb), F32),
                pltpu.SemaphoreType.DMA((4,)),
                pltpu.SemaphoreType.REGULAR((3,)),
                pltpu.SemaphoreType.REGULAR((2, 8)),
                pltpu.SemaphoreType.DMA((2, 4)),
                pltpu.SemaphoreType.DMA((2, 4)),
                pltpu.SemaphoreType.DMA((2, 8)),
                pltpu.SemaphoreType.DMA((2, 8)),
                pltpu.SemaphoreType.DMA((n_energy,)),
                pltpu.SemaphoreType.DMA((n_energy,)),
                pltpu.SemaphoreType.DMA((8,)),
            ],
            compiler_params=pltpu.CompilerParams(collective_id=0, has_side_effects=True, vmem_limit_bytes=14 * 2**20),
            name="self_energy",
        )(
            *(
                pltpu.with_memory_space_constraint(x, pltpu.HBM)
                for x in (
                    neighbours,
                    jnp.transpose(phonon, (0, 2, 1)),
                    green,
                    coupling.reshape(rows, orb, orb),
                )
            )
        )
        return sigma, rates

    return jax.shard_map(
        per_device,
        mesh=mesh,
        in_specs=(
            P(None, "energy", "atom", None, None),
            P("atom", None, None, None),
            P("atom", None, None),
            P("atom", None),
        ),
        out_specs=(P(None, "energy", "atom", None, None), P("atom", None)),
        check_vma=False,
    )
```

```python
import functools

import jax
import jax.numpy as jnp
from jax import lax
from jax.experimental import pallas as pl
from jax.experimental.pallas import tpu as pltpu
from jax.sharding import PartitionSpec as P

MESH = pl.DeviceIdType.MESH
F32 = jnp.float32
BF16 = jnp.bfloat16
Z_GROUPS = 4


def split(x):
    high = x.astype(BF16)
    low = (x - high.astype(F32)).astype(BF16)
    return high, low


def kernel(
    n_energy,
    n_atom,
    nbr,
    orb,
    nbr_hbm,
    ph_hbm,
    green,
    coupling,
    sigma_out,
    rates_out,
    nbr_ref,
    ph_ref,
    gbuf,
    cbuf,
    cleft,
    cright,
    gs,
    tbuf,
    own,
    send_next,
    send_prev,
    from_prev,
    from_next,
    gt,
    rsrc,
    rslots,
    local_sem,
    ready,
    known,
    a_send,
    a_recv,
    u_send,
    u_recv,
    r_send,
    r_recv,
    o_sem,
):
    ei = lax.axis_index("energy")
    ai = lax.axis_index("atom")
    nxt_a, prv_a = lax.rem(ai + 1, n_atom), lax.rem(ai + n_atom - 1, n_atom)
    nxt_e, prv_e = lax.rem(ei + 1, n_energy), lax.rem(ei + n_energy - 1, n_energy)

    group = lax.rem(ai, Z_GROUPS)
    first_group, last_group = group == 0, group == Z_GROUPS - 1
    barrier = pltpu.get_barrier_semaphore()

    def greet(sem, axis, peer):
        pl.semaphore_signal(sem, inc=1, device_id={axis: peer}, device_id_type=MESH)

    greet(barrier, "energy", prv_e)

    @pl.when(jnp.logical_not(last_group))
    def _():
        greet(barrier, "atom", nxt_a)

    @pl.when(first_group)
    def _():
        greet(barrier, "atom", prv_a)

    load_n = pltpu.make_async_copy(nbr_hbm, nbr_ref, local_sem.at[2])
    load_p = pltpu.make_async_copy(ph_hbm, ph_ref, local_sem.at[3])
    load_c = pltpu.make_async_copy(coupling, cbuf, local_sem.at[0])
    load_g = pltpu.make_async_copy(green, gbuf.at[:, :, pl.ds(2, 2)], local_sem.at[1])
    load_n.start()
    load_p.start()
    load_c.start()
    load_g.start()

    not_last, not_first = ai < n_atom - 1, ai > 0

    def atom_copy(c, e, up):
        return pltpu.make_async_remote_copy(
            src_ref=green.at[c, e],
            dst_ref=gbuf.at[c, e, pl.ds(0 if up else 4, 2)],
            send_sem=a_send.at[int(up), c * 2 + e],
            recv_sem=a_recv.at[int(up), c * 2 + e],
            device_id={"atom": nxt_a if up else prv_a},
            device_id_type=MESH,
        )

    def send_up():
        @pl.when(not_last)
        def _():
            for c in range(2):
                for e in range(2):
                    atom_copy(c, e, True).start()

    def send_down(c, e):
        @pl.when(not_first)
        def _():
            atom_copy(c, e, False).start()

    @pl.when(first_group)
    def _():
        pl.semaphore_wait(barrier, 1)

    @pl.when(jnp.logical_and(jnp.logical_not(first_group), jnp.logical_not(last_group)))
    def _():
        pl.semaphore_wait(barrier, 2)

    @pl.when(last_group)
    def _():
        pl.semaphore_wait(barrier, 3)
        greet(ready.at[0], "atom", nxt_a)
        send_up()

    greet(ready.at[2], "energy", nxt_e)

    @pl.when(jnp.logical_not(first_group))
    def _():
        greet(ready.at[1], "atom", prv_a)
        for c in range(2):
            for e in range(2):
                send_down(c, e)

    @pl.when(first_group)
    def _():
        pl.semaphore_wait(ready.at[1], 1)
        send_up()

    load_c.wait()

    def prepare(i, carry):
        mat = cbuf[i]
        high, low = split(mat)
        cleft[i, :, :orb] = high
        cleft[i, :, orb:] = low
        high, low = split(mat.T)
        for row in range(2):
            cright[i, row * orb : (row + 1) * orb, :orb] = high
            cright[i, row * orb : (row + 1) * orb, orb:] = low
        return carry

    lax.fori_loop(0, 2 * nbr, prepare, 0)

    @pl.when(jnp.logical_and(jnp.logical_not(first_group), jnp.logical_not(last_group)))
    def _():
        pl.semaphore_wait(ready.at[1], 1)
        send_up()

    @pl.when(first_group)
    def _():
        pl.semaphore_wait(ready.at[0], 1)
        for c in range(2):
            for e in range(2):
                send_down(c, e)

    pl.semaphore_wait(ready.at[2], 1)

    def tell(r):
        reach = 2**r
        for side, peer in enumerate((ei + reach, ei + n_energy - reach)):
            pl.semaphore_signal(
                known.at[side, r],
                inc=1,
                device_id={"energy": lax.rem(peer, n_energy)},
                device_id_type=MESH,
            )

    def hear(r):
        pl.semaphore_wait(known.at[0, r], 1)
        pl.semaphore_wait(known.at[1, r], 1)

    rounds = (n_energy // 2 - 1).bit_length()
    tell(0)
    load_g.wait()

    def turn(i, carry):
        c, e, a = i // 4, (i // 2) % 2, i % 2
        gt[c, e, a] = gbuf[c, e, 2 + a].T
        return carry

    lax.fori_loop(0, 8, turn, 0)
    load_n.wait()
    load_p.wait()
    for r in range(1, rounds):
        hear(r - 1)
        tell(r)
    hear(rounds - 1)

    def energy_copy(c, e, a, up):
        index = (c * 2 + e) * 2 + a
        return pltpu.make_async_remote_copy(
            src_ref=(send_next if up else send_prev).at[c, e, a],
            dst_ref=(from_prev if up else from_next).at[c, e, a],
            send_sem=u_send.at[int(up), index],
            recv_sem=u_recv.at[int(up), index],
            device_id={"energy": nxt_e if up else prv_e},
            device_id_type=MESH,
        )

    first = ai * 2

    def fill(c, e):
        def body(b, carry):
            high, low = split(gbuf[c, e, b])
            for row in range(2):
                gs[b, row * orb : (row + 1) * orb, :orb] = high
                gs[b, row * orb : (row + 1) * orb, orb:] = low
            return carry

        lax.fori_loop(0, 6, body, 0)

    def products(a):
        for j in range(nbr):
            i = a * nbr + j
            near = jnp.clip(nbr_ref[a, j] - first + 2, 0, 5)
            both = jnp.dot(cleft[i], gs[near], preferred_element_type=F32)
            high, low = split(both[:, :orb] + both[:, orb:])
            inner = jnp.concatenate([high, low], axis=1)
            both = jnp.dot(inner, cright[i], preferred_element_type=F32)
            tbuf[j] = both[:, :orb] + both[:, orb:]

    def mix(a, targets):
        weights = [[ph_ref[a, k, j] for k in range(4)] for j in range(nbr)]
        rows = 32

        def body(r, carry):
            at = pl.ds(pl.multiple_of(r * rows, rows), rows)
            terms = [tbuf[j, at, :] for j in range(nbr)]
            for k in range(4):
                ref, add = targets[k]
                total = weights[0][k] * terms[0]
                for j in range(1, nbr):
                    total = total + weights[j][k] * terms[j]
                if add:
                    total = total + ref[at, :]
                ref[at, :] = total
            return carry

        lax.fori_loop(0, orb // rows, body, 0)

    def one_c(c, carry):
        for e in range(2):
            @pl.when(not_first)
            def _():
                atom_copy(c, e, True).wait_recv()

            @pl.when(not_last)
            def _():
                atom_copy(c, e, False).wait_recv()

            fill(c, e)

            def one_a(a, inner_carry):
                products(a)
                if e == 0:
                    mix(
                        a,
                        (
                            (send_next.at[c, 0, a], False),
                            (own.at[c, 1, a], False),
                            (send_prev.at[c, 1, a], False),
                            (send_prev.at[c, 0, a], False),
                        ),
                    )
                    energy_copy(c, 0, a, False).start()
                else:
                    mix(
                        a,
                        (
                            (send_next.at[c, 1, a], False),
                            (send_next.at[c, 0, a], True),
                            (own.at[c, 0, a], False),
                            (send_prev.at[c, 1, a], True),
                        ),
                    )
                    energy_copy(c, 0, a, True).start()
                    energy_copy(c, 1, a, True).start()
                    energy_copy(c, 1, a, False).start()
                return inner_carry

            lax.fori_loop(0, 2, one_a, 0)

        return carry

    lax.fori_loop(0, 2, one_c, 0)

    has_prev, has_next = ei > 0, ei < n_energy - 1

    def out_copy(c, e, a):
        return pltpu.make_async_copy(
            own.at[c, e, a], sigma_out.at[c, e, a], o_sem.at[(c * 2 + e) * 2 + a]
        )

    for a in range(2):
        total = jnp.zeros((orb, orb), F32)
        for c in range(2):
            for e in range(2):
                energy_copy(c, e, a, True).wait_recv()
                energy_copy(c, e, a, False).wait_recv()
                block = own[c, e, a]
                block = block + jnp.where(has_prev, from_prev[c, e, a], 0.0)
                block = block + jnp.where(has_next, from_next[c, e, a], 0.0)
                own[c, e, a] = block
                term = block * gt[c, e, a]
                total = total + term if c == 0 else total - term
                out_copy(c, e, a).start()
        rsrc[a : a + 1, :] = jnp.sum(total.T, axis=0, keepdims=True)

    def rate_copy(sender, target):
        return pltpu.make_async_remote_copy(
            src_ref=rsrc,
            dst_ref=rslots.at[sender],
            send_sem=r_send.at[target],
            recv_sem=r_recv.at[sender],
            device_id={"energy": target},
            device_id_type=MESH,
        )

    def send_rate(p, carry):
        rate_copy(ei, lax.rem(ei + p, n_energy)).start()
        return carry

    lax.fori_loop(1, n_energy, send_rate, 0)
    rslots[ei] = rsrc[...]

    for c in range(2):
        for e in range(2):
            @pl.when(not_last)
            def _():
                atom_copy(c, e, True).wait_send()

            @pl.when(not_first)
            def _():
                atom_copy(c, e, False).wait_send()

            for a in range(2):
                energy_copy(c, e, a, True).wait_send()
                energy_copy(c, e, a, False).wait_send()
                out_copy(c, e, a).wait()

    def wait_rate_send(p, carry):
        rate_copy(ei, lax.rem(ei + p, n_energy)).wait_send()
        return carry

    lax.fori_loop(1, n_energy, wait_rate_send, 0)

    def wait_rate(p, carry):
        peer = lax.rem(ei + p, n_energy)
        rate_copy(peer, peer).wait_recv()
        return carry

    lax.fori_loop(1, n_energy, wait_rate, 0)
    total = rslots[0]
    for s in range(1, n_energy):
        total = total + rslots[s]
    rates_out[...] = total * (1.0 / (4.0 * 2 * n_energy))


def solution(mesh):
    n_energy, n_atom = mesh.shape["energy"], mesh.shape["atom"]

    def per_device(green, coupling, phonon, neighbours):
        orb, nbr = green.shape[-1], coupling.shape[1]
        rows = 2 * nbr
        whole = (2, 2, 2, orb, orb)
        any_space = pl.BlockSpec(memory_space=pl.ANY)
        sigma, rates = pl.pallas_call(
            functools.partial(kernel, n_energy, n_atom, nbr, orb),
            out_shape=(
                jax.ShapeDtypeStruct(whole, F32),
                jax.ShapeDtypeStruct((2, orb), F32),
            ),
            in_specs=[any_space] * 4,
            out_specs=(any_space, pl.BlockSpec(memory_space=pltpu.VMEM)),
            scratch_shapes=[
                pltpu.SMEM((2, nbr), jnp.int32),
                pltpu.SMEM((2, 4, nbr), F32),
                pltpu.VMEM((2, 2, 6, orb, orb), F32),
                pltpu.VMEM((rows, orb, orb), F32),
                pltpu.VMEM((rows, orb, 2 * orb), BF16),
                pltpu.VMEM((rows, 2 * orb, 2 * orb), BF16),
                pltpu.VMEM((6, 2 * orb, 2 * orb), BF16),
                pltpu.VMEM((nbr, orb, orb), F32),
                pltpu.VMEM(whole, F32),
                pltpu.VMEM(whole, F32),
                pltpu.VMEM(whole, F32),
                pltpu.VMEM(whole, F32),
                pltpu.VMEM(whole, F32),
                pltpu.VMEM(whole, F32),
                pltpu.VMEM((2, orb), F32),
                pltpu.VMEM((n_energy, 2, orb), F32),
                pltpu.SemaphoreType.DMA((4,)),
                pltpu.SemaphoreType.REGULAR((3,)),
                pltpu.SemaphoreType.REGULAR((2, 8)),
                pltpu.SemaphoreType.DMA((2, 4)),
                pltpu.SemaphoreType.DMA((2, 4)),
                pltpu.SemaphoreType.DMA((2, 8)),
                pltpu.SemaphoreType.DMA((2, 8)),
                pltpu.SemaphoreType.DMA((n_energy,)),
                pltpu.SemaphoreType.DMA((n_energy,)),
                pltpu.SemaphoreType.DMA((8,)),
            ],
            compiler_params=pltpu.CompilerParams(collective_id=0, has_side_effects=True, vmem_limit_bytes=14 * 2**20),
            name="self_energy",
        )(
            *(
                pltpu.with_memory_space_constraint(x, pltpu.HBM)
                for x in (
                    neighbours,
                    jnp.transpose(phonon, (0, 2, 1)),
                    green,
                    coupling.reshape(rows, orb, orb),
                )
            )
        )
        return sigma, rates

    return jax.shard_map(
        per_device,
        mesh=mesh,
        in_specs=(
            P(None, "energy", "atom", None, None),
            P("atom", None, None, None),
            P("atom", None, None),
            P("atom", None),
        ),
        out_specs=(P(None, "energy", "atom", None, None), P("atom", None)),
        check_vma=False,
    )
```

```python
import functools

import jax
import jax.numpy as jnp
from jax import lax
from jax.experimental import pallas as pl
from jax.experimental.pallas import tpu as pltpu
from jax.sharding import PartitionSpec as P

MESH = pl.DeviceIdType.MESH
F32 = jnp.float32
BF16 = jnp.bfloat16
Z_GROUPS = 4


def split(x):
    high = x.astype(BF16)
    low = (x - high.astype(F32)).astype(BF16)
    return high, low


def kernel(
    n_energy,
    n_atom,
    nbr,
    orb,
    nbr_hbm,
    ph_hbm,
    green,
    coupling,
    sigma_out,
    rates_out,
    nbr_ref,
    ph_ref,
    gbuf,
    cbuf,
    cleft,
    cright,
    gs,
    tbuf,
    own,
    send_next,
    send_prev,
    from_prev,
    from_next,
    gt,
    rsrc,
    rslots,
    local_sem,
    ready,
    known,
    a_send,
    a_recv,
    u_send,
    u_recv,
    r_send,
    r_recv,
    o_sem,
):
    ei = lax.axis_index("energy")
    ai = lax.axis_index("atom")
    nxt_a, prv_a = lax.rem(ai + 1, n_atom), lax.rem(ai + n_atom - 1, n_atom)
    nxt_e, prv_e = lax.rem(ei + 1, n_energy), lax.rem(ei + n_energy - 1, n_energy)

    group = lax.rem(ai, Z_GROUPS)
    first_group, last_group = group == 0, group == Z_GROUPS - 1
    barrier = pltpu.get_barrier_semaphore()

    def greet(sem, axis, peer):
        pl.semaphore_signal(sem, inc=1, device_id={axis: peer}, device_id_type=MESH)

    greet(barrier, "energy", prv_e)

    @pl.when(jnp.logical_not(last_group))
    def _():
        greet(barrier, "atom", nxt_a)

    @pl.when(first_group)
    def _():
        greet(barrier, "atom", prv_a)

    load_n = pltpu.make_async_copy(nbr_hbm, nbr_ref, local_sem.at[2])
    load_p = pltpu.make_async_copy(ph_hbm, ph_ref, local_sem.at[3])
    load_c = pltpu.make_async_copy(coupling, cbuf, local_sem.at[0])
    load_g = pltpu.make_async_copy(green, gbuf.at[:, :, pl.ds(2, 2)], local_sem.at[1])
    load_n.start()
    load_p.start()
    load_c.start()
    load_g.start()

    not_last, not_first = ai < n_atom - 1, ai > 0

    def atom_copy(c, e, up):
        return pltpu.make_async_remote_copy(
            src_ref=green.at[c, e],
            dst_ref=gbuf.at[c, e, pl.ds(0 if up else 4, 2)],
            send_sem=a_send.at[int(up), c * 2 + e],
            recv_sem=a_recv.at[int(up), c * 2 + e],
            device_id={"atom": nxt_a if up else prv_a},
            device_id_type=MESH,
        )

    def send_up_last():
        @pl.when(not_last)
        def _():
            atom_copy(1, 1, True).start()

    def send_up():
        @pl.when(not_last)
        def _():
            atom_copy(0, 0, True).start()
            atom_copy(0, 1, True).start()
            atom_copy(1, 0, True).start()

        @pl.when(not_first)
        def _():
            send_up_last()

    def send_down(c, e):
        @pl.when(not_first)
        def _():
            atom_copy(c, e, False).start()

    @pl.when(first_group)
    def _():
        pl.semaphore_wait(barrier, 1)

    @pl.when(jnp.logical_and(jnp.logical_not(first_group), jnp.logical_not(last_group)))
    def _():
        pl.semaphore_wait(barrier, 2)

    @pl.when(last_group)
    def _():
        pl.semaphore_wait(barrier, 3)
        greet(ready.at[0], "atom", nxt_a)
        send_up()

    greet(ready.at[2], "energy", nxt_e)

    @pl.when(jnp.logical_not(first_group))
    def _():
        greet(ready.at[1], "atom", prv_a)
        for c in range(2):
            for e in range(2):
                send_down(c, e)

    @pl.when(first_group)
    def _():
        pl.semaphore_wait(ready.at[1], 1)
        send_up()

    load_c.wait()

    def prepare(i, carry):
        mat = cbuf[i]
        high, low = split(mat)
        cleft[i, :, :orb] = high
        cleft[i, :, orb:] = low
        high, low = split(mat.T)
        for row in range(2):
            cright[i, row * orb : (row + 1) * orb, :orb] = high
            cright[i, row * orb : (row + 1) * orb, orb:] = low
        return carry

    lax.fori_loop(0, 2 * nbr, prepare, 0)

    @pl.when(jnp.logical_and(jnp.logical_not(first_group), jnp.logical_not(last_group)))
    def _():
        pl.semaphore_wait(ready.at[1], 1)
        send_up()

    @pl.when(first_group)
    def _():
        pl.semaphore_wait(ready.at[0], 1)
        send_down(0, 0)
        send_down(0, 1)
        send_down(1, 0)

    pl.semaphore_wait(ready.at[2], 1)

    def tell(r):
        reach = 2**r
        for side, peer in enumerate((ei + reach, ei + n_energy - reach)):
            pl.semaphore_signal(
                known.at[side, r],
                inc=1,
                device_id={"energy": lax.rem(peer, n_energy)},
                device_id_type=MESH,
            )

    def hear(r):
        pl.semaphore_wait(known.at[0, r], 1)
        pl.semaphore_wait(known.at[1, r], 1)

    rounds = (n_energy // 2 - 1).bit_length()
    tell(0)
    load_g.wait()

    def turn(i, carry):
        c, e, a = i // 4, (i // 2) % 2, i % 2
        gt[c, e, a] = gbuf[c, e, 2 + a].T
        return carry

    lax.fori_loop(0, 8, turn, 0)
    load_n.wait()
    load_p.wait()
    for r in range(1, rounds):
        hear(r - 1)
        tell(r)
    hear(rounds - 1)

    def energy_copy(c, e, a, up):
        index = (c * 2 + e) * 2 + a
        return pltpu.make_async_remote_copy(
            src_ref=(send_next if up else send_prev).at[c, e, a],
            dst_ref=(from_prev if up else from_next).at[c, e, a],
            send_sem=u_send.at[int(up), index],
            recv_sem=u_recv.at[int(up), index],
            device_id={"energy": nxt_e if up else prv_e},
            device_id_type=MESH,
        )

    first = ai * 2

    def fill(c, e):
        def body(b, carry):
            high, low = split(gbuf[c, e, b])
            for row in range(2):
                gs[b, row * orb : (row + 1) * orb, :orb] = high
                gs[b, row * orb : (row + 1) * orb, orb:] = low
            return carry

        lax.fori_loop(0, 6, body, 0)

    def products(a):
        for j in range(nbr):
            i = a * nbr + j
            near = jnp.clip(nbr_ref[a, j] - first + 2, 0, 5)
            both = jnp.dot(cleft[i], gs[near], preferred_element_type=F32)
            high, low = split(both[:, :orb] + both[:, orb:])
            inner = jnp.concatenate([high, low], axis=1)
            both = jnp.dot(inner, cright[i], preferred_element_type=F32)
            tbuf[j] = both[:, :orb] + both[:, orb:]

    def mix(a, targets):
        weights = [[ph_ref[a, k, j] for k in range(4)] for j in range(nbr)]
        rows = 32

        def body(r, carry):
            at = pl.ds(pl.multiple_of(r * rows, rows), rows)
            terms = [tbuf[j, at, :] for j in range(nbr)]
            for k in range(4):
                ref, add = targets[k]
                total = weights[0][k] * terms[0]
                for j in range(1, nbr):
                    total = total + weights[j][k] * terms[j]
                if add:
                    total = total + ref[at, :]
                ref[at, :] = total
            return carry

        lax.fori_loop(0, orb // rows, body, 0)

    def one_c(c, carry):
        for e in range(2):
            @pl.when(not_first)
            def _():
                atom_copy(c, e, True).wait_recv()

            @pl.when(not_last)
            def _():
                atom_copy(c, e, False).wait_recv()

            fill(c, e)

            def one_a(a, inner_carry):
                products(a)
                if e == 0:
                    mix(
                        a,
                        (
                            (send_next.at[c, 0, a], False),
                            (own.at[c, 1, a], False),
                            (send_prev.at[c, 1, a], False),
                            (send_prev.at[c, 0, a], False),
                        ),
                    )
                    energy_copy(c, 0, a, False).start()
                else:
                    mix(
                        a,
                        (
                            (send_next.at[c, 1, a], False),
                            (send_next.at[c, 0, a], True),
                            (own.at[c, 0, a], False),
                            (send_prev.at[c, 1, a], True),
                        ),
                    )
                    energy_copy(c, 0, a, True).start()
                    energy_copy(c, 1, a, True).start()
                    energy_copy(c, 1, a, False).start()
                return inner_carry

            lax.fori_loop(0, 2, one_a, 0)
            if e == 1:
                @pl.when(jnp.logical_and(c == 0, jnp.logical_not(not_first)))
                def _():
                    send_up_last()

        return carry

    lax.fori_loop(0, 2, one_c, 0)

    @pl.when(first_group)
    def _():
        send_down(1, 1)

    has_prev, has_next = ei > 0, ei < n_energy - 1

    def out_copy(c, e, a):
        return pltpu.make_async_copy(
            own.at[c, e, a], sigma_out.at[c, e, a], o_sem.at[(c * 2 + e) * 2 + a]
        )

    for a in range(2):
        total = jnp.zeros((orb, orb), F32)
        for c in range(2):
            for e in range(2):
                energy_copy(c, e, a, True).wait_recv()
                energy_copy(c, e, a, False).wait_recv()
                block = own[c, e, a]
                block = block + jnp.where(has_prev, from_prev[c, e, a], 0.0)
                block = block + jnp.where(has_next, from_next[c, e, a], 0.0)
                own[c, e, a] = block
                term = block * gt[c, e, a]
                total = total + term if c == 0 else total - term
                out_copy(c, e, a).start()
        rsrc[a : a + 1, :] = jnp.sum(total.T, axis=0, keepdims=True)

    def rate_copy(sender, target):
        return pltpu.make_async_remote_copy(
            src_ref=rsrc,
            dst_ref=rslots.at[sender],
            send_sem=r_send.at[target],
            recv_sem=r_recv.at[sender],
            device_id={"energy": target},
            device_id_type=MESH,
        )

    def send_rate(p, carry):
        rate_copy(ei, lax.rem(ei + p, n_energy)).start()
        return carry

    lax.fori_loop(1, n_energy, send_rate, 0)
    rslots[ei] = rsrc[...]

    for c in range(2):
        for e in range(2):
            @pl.when(not_last)
            def _():
                atom_copy(c, e, True).wait_send()

            @pl.when(not_first)
            def _():
                atom_copy(c, e, False).wait_send()

            for a in range(2):
                energy_copy(c, e, a, True).wait_send()
                energy_copy(c, e, a, False).wait_send()
                out_copy(c, e, a).wait()

    def wait_rate_send(p, carry):
        rate_copy(ei, lax.rem(ei + p, n_energy)).wait_send()
        return carry

    lax.fori_loop(1, n_energy, wait_rate_send, 0)

    def wait_rate(p, carry):
        peer = lax.rem(ei + p, n_energy)
        rate_copy(peer, peer).wait_recv()
        return carry

    lax.fori_loop(1, n_energy, wait_rate, 0)
    total = rslots[0]
    for s in range(1, n_energy):
        total = total + rslots[s]
    rates_out[...] = total * (1.0 / (4.0 * 2 * n_energy))


def solution(mesh):
    n_energy, n_atom = mesh.shape["energy"], mesh.shape["atom"]

    def per_device(green, coupling, phonon, neighbours):
        orb, nbr = green.shape[-1], coupling.shape[1]
        rows = 2 * nbr
        whole = (2, 2, 2, orb, orb)
        any_space = pl.BlockSpec(memory_space=pl.ANY)
        sigma, rates = pl.pallas_call(
            functools.partial(kernel, n_energy, n_atom, nbr, orb),
            out_shape=(
                jax.ShapeDtypeStruct(whole, F32),
                jax.ShapeDtypeStruct((2, orb), F32),
            ),
            in_specs=[any_space] * 4,
            out_specs=(any_space, pl.BlockSpec(memory_space=pltpu.VMEM)),
            scratch_shapes=[
                pltpu.SMEM((2, nbr), jnp.int32),
                pltpu.SMEM((2, 4, nbr), F32),
                pltpu.VMEM((2, 2, 6, orb, orb), F32),
                pltpu.VMEM((rows, orb, orb), F32),
                pltpu.VMEM((rows, orb, 2 * orb), BF16),
                pltpu.VMEM((rows, 2 * orb, 2 * orb), BF16),
                pltpu.VMEM((6, 2 * orb, 2 * orb), BF16),
                pltpu.VMEM((nbr, orb, orb), F32),
                pltpu.VMEM(whole, F32),
                pltpu.VMEM(whole, F32),
                pltpu.VMEM(whole, F32),
                pltpu.VMEM(whole, F32),
                pltpu.VMEM(whole, F32),
                pltpu.VMEM(whole, F32),
                pltpu.VMEM((2, orb), F32),
                pltpu.VMEM((n_energy, 2, orb), F32),
                pltpu.SemaphoreType.DMA((4,)),
                pltpu.SemaphoreType.REGULAR((3,)),
                pltpu.SemaphoreType.REGULAR((2, 8)),
                pltpu.SemaphoreType.DMA((2, 4)),
                pltpu.SemaphoreType.DMA((2, 4)),
                pltpu.SemaphoreType.DMA((2, 8)),
                pltpu.SemaphoreType.DMA((2, 8)),
                pltpu.SemaphoreType.DMA((n_energy,)),
                pltpu.SemaphoreType.DMA((n_energy,)),
                pltpu.SemaphoreType.DMA((8,)),
            ],
            compiler_params=pltpu.CompilerParams(collective_id=0, has_side_effects=True, vmem_limit_bytes=14 * 2**20),
            name="self_energy",
        )(
            *(
                pltpu.with_memory_space_constraint(x, pltpu.HBM)
                for x in (
                    neighbours,
                    jnp.transpose(phonon, (0, 2, 1)),
                    green,
                    coupling.reshape(rows, orb, orb),
                )
            )
        )
        return sigma, rates

    return jax.shard_map(
        per_device,
        mesh=mesh,
        in_specs=(
            P(None, "energy", "atom", None, None),
            P("atom", None, None, None),
            P("atom", None, None),
            P("atom", None),
        ),
        out_specs=(P(None, "energy", "atom", None, None), P("atom", None)),
        check_vma=False,
    )
```

```python
import functools

import jax
import jax.numpy as jnp
from jax import lax
from jax.experimental import pallas as pl
from jax.experimental.pallas import tpu as pltpu
from jax.sharding import PartitionSpec as P

MESH = pl.DeviceIdType.MESH
F32 = jnp.float32
BF16 = jnp.bfloat16
Z_GROUPS = 4


def split(x):
    high = x.astype(BF16)
    low = (x - high.astype(F32)).astype(BF16)
    return high, low


def kernel(
    n_energy,
    n_atom,
    nbr,
    orb,
    nbr_hbm,
    ph_hbm,
    green,
    coupling,
    sigma_out,
    rates_out,
    nbr_ref,
    ph_ref,
    gbuf,
    cbuf,
    cleft,
    cright,
    gs,
    tbuf,
    own,
    send_next,
    send_prev,
    from_prev,
    from_next,
    gt,
    rsrc,
    rslots,
    local_sem,
    ready,
    known,
    a_send,
    a_recv,
    u_send,
    u_recv,
    r_send,
    r_recv,
    o_sem,
):
    ei = lax.axis_index("energy")
    ai = lax.axis_index("atom")
    nxt_a, prv_a = lax.rem(ai + 1, n_atom), lax.rem(ai + n_atom - 1, n_atom)
    nxt_e, prv_e = lax.rem(ei + 1, n_energy), lax.rem(ei + n_energy - 1, n_energy)

    group = lax.rem(ai, Z_GROUPS)
    first_group, last_group = group == 0, group == Z_GROUPS - 1
    barrier = pltpu.get_barrier_semaphore()

    def greet(sem, axis, peer):
        pl.semaphore_signal(sem, inc=1, device_id={axis: peer}, device_id_type=MESH)

    greet(barrier, "energy", prv_e)

    @pl.when(jnp.logical_not(last_group))
    def _():
        greet(barrier, "atom", nxt_a)

    @pl.when(jnp.logical_or(first_group, group == 1))
    def _():
        greet(barrier, "atom", prv_a)

    load_n = pltpu.make_async_copy(nbr_hbm, nbr_ref, local_sem.at[2])
    load_p = pltpu.make_async_copy(ph_hbm, ph_ref, local_sem.at[3])
    load_c = pltpu.make_async_copy(coupling, cbuf, local_sem.at[0])
    load_g = pltpu.make_async_copy(green, gbuf.at[:, :, pl.ds(2, 2)], local_sem.at[1])
    load_n.start()
    load_p.start()
    load_c.start()
    load_g.start()

    not_last, not_first = ai < n_atom - 1, ai > 0

    def atom_copy(c, e, up):
        return pltpu.make_async_remote_copy(
            src_ref=green.at[c, e],
            dst_ref=gbuf.at[c, e, pl.ds(0 if up else 4, 2)],
            send_sem=a_send.at[int(up), c * 2 + e],
            recv_sem=a_recv.at[int(up), c * 2 + e],
            device_id={"atom": nxt_a if up else prv_a},
            device_id_type=MESH,
        )

    def send_up():
        @pl.when(not_last)
        def _():
            for c in range(2):
                for e in range(2):
                    atom_copy(c, e, True).start()

    def send_down(c, e):
        @pl.when(not_first)
        def _():
            atom_copy(c, e, False).start()

    @pl.when(jnp.logical_not(last_group))
    def _():
        pl.semaphore_wait(barrier, 2)

    @pl.when(last_group)
    def _():
        pl.semaphore_wait(barrier, 3)
        greet(ready.at[0], "atom", nxt_a)
        send_up()

    greet(ready.at[2], "energy", nxt_e)

    @pl.when(jnp.logical_not(first_group))
    def _():
        @pl.when(group > 1)
        def _():
            greet(ready.at[1], "atom", prv_a)

        for c in range(2):
            for e in range(2):
                send_down(c, e)

    @pl.when(first_group)
    def _():
        send_up()

    load_c.wait()

    def prepare(i, carry):
        mat = cbuf[i]
        high, low = split(mat)
        cleft[i, :, :orb] = high
        cleft[i, :, orb:] = low
        high, low = split(mat.T)
        for row in range(2):
            cright[i, row * orb : (row + 1) * orb, :orb] = high
            cright[i, row * orb : (row + 1) * orb, orb:] = low
        return carry

    lax.fori_loop(0, 2 * nbr, prepare, 0)

    @pl.when(jnp.logical_and(jnp.logical_not(first_group), jnp.logical_not(last_group)))
    def _():
        pl.semaphore_wait(ready.at[1], 1)
        send_up()

    @pl.when(first_group)
    def _():
        pl.semaphore_wait(ready.at[0], 1)
        send_down(0, 0)
        send_down(0, 1)
        send_down(1, 0)

    pl.semaphore_wait(ready.at[2], 1)

    def tell(r):
        reach = 2**r
        for side, peer in enumerate((ei + reach, ei + n_energy - reach)):
            pl.semaphore_signal(
                known.at[side, r],
                inc=1,
                device_id={"energy": lax.rem(peer, n_energy)},
                device_id_type=MESH,
            )

    def hear(r):
        pl.semaphore_wait(known.at[0, r], 1)
        pl.semaphore_wait(known.at[1, r], 1)

    rounds = (n_energy // 2 - 1).bit_length()
    tell(0)
    load_g.wait()

    def turn(i, carry):
        c, e, a = i // 4, (i // 2) % 2, i % 2
        gt[c, e, a] = gbuf[c, e, 2 + a].T
        return carry

    lax.fori_loop(0, 8, turn, 0)
    load_n.wait()
    load_p.wait()
    for r in range(1, rounds):
        hear(r - 1)
        tell(r)
    hear(rounds - 1)

    def energy_copy(c, e, a, up):
        index = (c * 2 + e) * 2 + a
        return pltpu.make_async_remote_copy(
            src_ref=(send_next if up else send_prev).at[c, e, a],
            dst_ref=(from_prev if up else from_next).at[c, e, a],
            send_sem=u_send.at[int(up), index],
            recv_sem=u_recv.at[int(up), index],
            device_id={"energy": nxt_e if up else prv_e},
            device_id_type=MESH,
        )

    first = ai * 2

    def fill(c, e):
        def body(b, carry):
            high, low = split(gbuf[c, e, b])
            for row in range(2):
                gs[b, row * orb : (row + 1) * orb, :orb] = high
                gs[b, row * orb : (row + 1) * orb, orb:] = low
            return carry

        lax.fori_loop(0, 6, body, 0)

    def products(a):
        for j in range(nbr):
            i = a * nbr + j
            near = jnp.clip(nbr_ref[a, j] - first + 2, 0, 5)
            both = jnp.dot(cleft[i], gs[near], preferred_element_type=F32)
            high, low = split(both[:, :orb] + both[:, orb:])
            inner = jnp.concatenate([high, low], axis=1)
            both = jnp.dot(inner, cright[i], preferred_element_type=F32)
            tbuf[j] = both[:, :orb] + both[:, orb:]

    def mix(a, targets):
        weights = [[ph_ref[a, k, j] for k in range(4)] for j in range(nbr)]
        rows = 32

        def body(r, carry):
            at = pl.ds(pl.multiple_of(r * rows, rows), rows)
            terms = [tbuf[j, at, :] for j in range(nbr)]
            for k in range(4):
                ref, add = targets[k]
                total = weights[0][k] * terms[0]
                for j in range(1, nbr):
                    total = total + weights[j][k] * terms[j]
                if add:
                    total = total + ref[at, :]
                ref[at, :] = total
            return carry

        lax.fori_loop(0, orb // rows, body, 0)

    def one_c(c, carry):
        for e in range(2):
            @pl.when(not_first)
            def _():
                atom_copy(c, e, True).wait_recv()

            @pl.when(not_last)
            def _():
                atom_copy(c, e, False).wait_recv()

            fill(c, e)

            def one_a(a, inner_carry):
                products(a)
                if e == 0:
                    mix(
                        a,
                        (
                            (send_next.at[c, 0, a], False),
                            (own.at[c, 1, a], False),
                            (send_prev.at[c, 1, a], False),
                            (send_prev.at[c, 0, a], False),
                        ),
                    )
                    energy_copy(c, 0, a, False).start()
                else:
                    mix(
                        a,
                        (
                            (send_next.at[c, 1, a], False),
                            (send_next.at[c, 0, a], True),
                            (own.at[c, 0, a], False),
                            (send_prev.at[c, 1, a], True),
                        ),
                    )
                    energy_copy(c, 0, a, True).start()
                    energy_copy(c, 1, a, True).start()
                    energy_copy(c, 1, a, False).start()
                return inner_carry

            lax.fori_loop(0, 2, one_a, 0)

        return carry

    lax.fori_loop(0, 2, one_c, 0)

    @pl.when(first_group)
    def _():
        send_down(1, 1)

    has_prev, has_next = ei > 0, ei < n_energy - 1

    def out_copy(c, e, a):
        return pltpu.make_async_copy(
            own.at[c, e, a], sigma_out.at[c, e, a], o_sem.at[(c * 2 + e) * 2 + a]
        )

    for a in range(2):
        total = jnp.zeros((orb, orb), F32)
        for c in range(2):
            for e in range(2):
                energy_copy(c, e, a, True).wait_recv()
                energy_copy(c, e, a, False).wait_recv()
                block = own[c, e, a]
                block = block + jnp.where(has_prev, from_prev[c, e, a], 0.0)
                block = block + jnp.where(has_next, from_next[c, e, a], 0.0)
                own[c, e, a] = block
                term = block * gt[c, e, a]
                total = total + term if c == 0 else total - term
                out_copy(c, e, a).start()
        rsrc[a : a + 1, :] = jnp.sum(total.T, axis=0, keepdims=True)

    def rate_copy(sender, target):
        return pltpu.make_async_remote_copy(
            src_ref=rsrc,
            dst_ref=rslots.at[sender],
            send_sem=r_send.at[target],
            recv_sem=r_recv.at[sender],
            device_id={"energy": target},
            device_id_type=MESH,
        )

    def send_rate(p, carry):
        rate_copy(ei, lax.rem(ei + p, n_energy)).start()
        return carry

    lax.fori_loop(1, n_energy, send_rate, 0)
    rslots[ei] = rsrc[...]

    for c in range(2):
        for e in range(2):
            @pl.when(not_last)
            def _():
                atom_copy(c, e, True).wait_send()

            @pl.when(not_first)
            def _():
                atom_copy(c, e, False).wait_send()

            for a in range(2):
                energy_copy(c, e, a, True).wait_send()
                energy_copy(c, e, a, False).wait_send()
                out_copy(c, e, a).wait()

    def wait_rate_send(p, carry):
        rate_copy(ei, lax.rem(ei + p, n_energy)).wait_send()
        return carry

    lax.fori_loop(1, n_energy, wait_rate_send, 0)

    def wait_rate(p, carry):
        peer = lax.rem(ei + p, n_energy)
        rate_copy(peer, peer).wait_recv()
        return carry

    lax.fori_loop(1, n_energy, wait_rate, 0)
    total = rslots[0]
    for s in range(1, n_energy):
        total = total + rslots[s]
    rates_out[...] = total * (1.0 / (4.0 * 2 * n_energy))


def solution(mesh):
    n_energy, n_atom = mesh.shape["energy"], mesh.shape["atom"]

    def per_device(green, coupling, phonon, neighbours):
        orb, nbr = green.shape[-1], coupling.shape[1]
        rows = 2 * nbr
        whole = (2, 2, 2, orb, orb)
        any_space = pl.BlockSpec(memory_space=pl.ANY)
        sigma, rates = pl.pallas_call(
            functools.partial(kernel, n_energy, n_atom, nbr, orb),
            out_shape=(
                jax.ShapeDtypeStruct(whole, F32),
                jax.ShapeDtypeStruct((2, orb), F32),
            ),
            in_specs=[any_space] * 4,
            out_specs=(any_space, pl.BlockSpec(memory_space=pltpu.VMEM)),
            scratch_shapes=[
                pltpu.SMEM((2, nbr), jnp.int32),
                pltpu.SMEM((2, 4, nbr), F32),
                pltpu.VMEM((2, 2, 6, orb, orb), F32),
                pltpu.VMEM((rows, orb, orb), F32),
                pltpu.VMEM((rows, orb, 2 * orb), BF16),
                pltpu.VMEM((rows, 2 * orb, 2 * orb), BF16),
                pltpu.VMEM((6, 2 * orb, 2 * orb), BF16),
                pltpu.VMEM((nbr, orb, orb), F32),
                pltpu.VMEM(whole, F32),
                pltpu.VMEM(whole, F32),
                pltpu.VMEM(whole, F32),
                pltpu.VMEM(whole, F32),
                pltpu.VMEM(whole, F32),
                pltpu.VMEM(whole, F32),
                pltpu.VMEM((2, orb), F32),
                pltpu.VMEM((n_energy, 2, orb), F32),
                pltpu.SemaphoreType.DMA((4,)),
                pltpu.SemaphoreType.REGULAR((3,)),
                pltpu.SemaphoreType.REGULAR((2, 8)),
                pltpu.SemaphoreType.DMA((2, 4)),
                pltpu.SemaphoreType.DMA((2, 4)),
                pltpu.SemaphoreType.DMA((2, 8)),
                pltpu.SemaphoreType.DMA((2, 8)),
                pltpu.SemaphoreType.DMA((n_energy,)),
                pltpu.SemaphoreType.DMA((n_energy,)),
                pltpu.SemaphoreType.DMA((8,)),
            ],
            compiler_params=pltpu.CompilerParams(collective_id=0, has_side_effects=True, vmem_limit_bytes=14 * 2**20),
            name="self_energy",
        )(
            *(
                pltpu.with_memory_space_constraint(x, pltpu.HBM)
                for x in (
                    neighbours,
                    jnp.transpose(phonon, (0, 2, 1)),
                    green,
                    coupling.reshape(rows, orb, orb),
                )
            )
        )
        return sigma, rates

    return jax.shard_map(
        per_device,
        mesh=mesh,
        in_specs=(
            P(None, "energy", "atom", None, None),
            P("atom", None, None, None),
            P("atom", None, None),
            P("atom", None),
        ),
        out_specs=(P(None, "energy", "atom", None, None), P("atom", None)),
        check_vma=False,
    )
```
